256 devices in a mesh: rows: 64 (over y_lo, z, x), blk: 4 (over y_hi, core).
Axes of the slice: x: 4, y: 4 (y_hi: 2, y_lo: 2; y = y_hi * 2 + y_lo), z: 8, core: 2. Of those that a mesh axis runs over, the one named last changes fastest.
Arguments:
- block_weight: bfloat16 [64, 4, 4, 64, 128, 128], P('rows', 'blk'), may hold values from 0.049804688 to 50
- block_row: int32 [64, 4, 4, 64], P('rows', 'blk'), may hold values from 0 to 15, as said below
- block_col: int32 [64, 4, 4, 64], P('rows', 'blk'), may hold values from 0 to 7, as said below
- block_count: int32 [64, 4, 4], P('rows', 'blk'), may hold values from 1 to 64, as said below
- block_samples: int32 [64, 4, 4, 64], P('rows', 'blk'), may hold values from 1 to 8
- row_degree: float32 [64, 4, 2048], P('rows', 'blk'), may hold values from 0.125 to 8
- col_degree: float32 [4, 1024], P('blk', 'rows'), may hold values from 1 to 8
- test_matrix: bfloat16 [4, 1024, 128], P('blk', 'rows'), may hold values from -6 to 6
Outputs:
- basis: float32 [64, 4, 2048, 128], P('rows', 'blk')
- triangle: float32 [128, 128], replicated
The draws below stay inside these ranges and needn't reach their ends.
Inputs may be any that keep to these rules, and one draw needn't show every extreme that they name: Within one band and slab, the slots k < 64 hold distinct (block_row, block_col) pairs. `block_col`: see block_row: pairs are distinct within one band and slab. `block_count`: some band and slab has all 64 slots live in every draw.
All inputs are finite; a program needn't handle non-finite values.
Results may differ from the reference program's by a relative error of at most 0.0065.
Values may be sent and summed in bfloat16 or wider, within the bound.
A program may use at most 64 MiB of HBM per device.

```python
import math
import jax
import jax.numpy as jnp
from jax import lax

BLK = 128
SKETCH = 128
RB_DEV = 16
SLAB_BLK = 8
CAP = 64
BAND = 2048
SLAB = 1024
N_ROWS = 64
N_BLK = 4


def coord_pairs(key):
    keys = jax.random.split(jax.random.fold_in(key, 11), N_ROWS * N_BLK * N_BLK)
    perms = jax.vmap(lambda k: jax.random.permutation(k, RB_DEV * SLAB_BLK)[:CAP])(keys)
    return perms.reshape(N_ROWS, N_BLK, N_BLK, CAP).astype(jnp.int32)


def draw_block_row(key, part):
    return coord_pairs(key) // SLAB_BLK


def draw_block_col(key, part):
    return coord_pairs(key) % SLAB_BLK


def draw_block_count(key, part):
    base = jax.random.randint(jax.random.fold_in(key, 5), (N_ROWS * N_BLK * N_BLK,), CAP // 4, CAP + 1)
    where = jax.random.randint(jax.random.fold_in(key, 6), (), 0, N_ROWS * N_BLK * N_BLK)
    base = base.at[where].set(CAP)
    return jnp.maximum(base, 1).reshape(N_ROWS, N_BLK, N_BLK).astype(jnp.int32)


def draw_row_degree(key, part):
    shape = (N_ROWS, N_BLK, BAND)
    base_deg = jnp.exp(jax.random.uniform(jax.random.fold_in(key, 22), shape, jnp.float32, 0.0, jnp.log(8.0)))
    band_total = N_ROWS * N_BLK
    band_place = jnp.arange(band_total, dtype=jnp.float32).reshape(N_ROWS, N_BLK, 1) / max(band_total - 1, 1)
    factor = jnp.exp2(-3.0 * band_place)
    return (base_deg * factor).astype(jnp.float32)


def place_ends(drawn, rng, least, largest):
    index_at = [jax.random.randint(jax.random.fold_in(rng, axis), (), 0, length) for axis, length in enumerate(drawn.shape)]
    longest = drawn.shape.index(max(drawn.shape))
    next_to = index_at[:longest] + [(index_at[longest] + 1) % drawn.shape[longest]] + index_at[longest + 1:]
    return drawn.at[tuple(index_at)].set(least).at[tuple(next_to)].set(largest)


def level_of(rng, shape, cuts, low, top_value):
    gain = 1.0
    for axis_at, parts in cuts:
        draws = jax.random.uniform(jax.random.fold_in(jax.random.fold_in(rng, 6), axis_at), (parts,), jnp.float32, low / len(cuts), top_value / len(cuts))
        gain = gain * jnp.repeat(jnp.exp(draws), shape[axis_at] // parts).reshape((-1,) + (1,) * (len(shape) - 1 - axis_at))
    return gain


def noise(rng, extent, deviation, limit, cuts=(), kind=jnp.bfloat16):
    factor_of = level_of(rng, extent, cuts, -0.22, 0.18) if cuts else 1.0
    values = jax.random.normal(rng, extent, jnp.float32) * deviation * factor_of
    return jnp.minimum(jnp.maximum(values, -limit), limit).astype(kind)


def setup_inputs(seed: int = 0) -> dict:
    streams_of = jax.random.split(jax.random.key(seed), 9)
    return {
        "block_weight": jnp.clip(jnp.exp(math.log(50.0) - 6.9116692 * jax.random.uniform(streams_of[0], (N_ROWS, N_BLK, N_BLK, CAP, BLK, BLK), jnp.float32) ** level_of(streams_of[0], (N_ROWS, N_BLK, N_BLK, CAP, BLK, BLK), ((0, 64), (1, 4)), -0.2, 0.2)), 0.049804688, 50.0).astype(jnp.bfloat16),
        "block_row": draw_block_row(jax.random.fold_in(streams_of[8], 71), 0),
        "block_col": draw_block_col(jax.random.fold_in(streams_of[8], 71), 0),
        "block_count": draw_block_count(jax.random.fold_in(streams_of[8], 71), 0),
        "block_samples": place_ends(jax.random.randint(streams_of[4], (N_ROWS, N_BLK, N_BLK, CAP), 1, 9), jax.random.fold_in(streams_of[4], 1), 1, 8).astype(jnp.int32),
        "row_degree": draw_row_degree(jax.random.fold_in(streams_of[8], 71), 0),
        "col_degree": jnp.clip(jnp.exp(math.log(8.0) - 2.0794415 * jax.random.uniform(streams_of[6], (N_BLK, SLAB), jnp.float32) ** level_of(streams_of[6], (N_BLK, SLAB), ((0, 4), (1, 64)), -0.2, 0.2)), 1.0, 8.0),
        "test_matrix": noise(streams_of[7], (N_BLK, SLAB, SKETCH), 1.0, 6.0, ((0, 4), (1, 64))),
    }


scale_factor = 16.0

def tile_update(running, weights, rows_idx, cols_idx, live_count, samples, row_deg, slab_rows, slab_deg):
    block_edge = weights.shape[-1]
    capacity = weights.shape[0]
    band_blocks = running.shape[0]
    slab_blocks = slab_rows.shape[0] // block_edge
    slab_tiles = slab_rows.reshape(slab_blocks, block_edge, slab_rows.shape[1])
    picked = slab_tiles[cols_idx].astype(jnp.float32)
    col_d = slab_deg.reshape(slab_blocks, block_edge)[cols_idx]
    row_d = row_deg.reshape(band_blocks, block_edge)[rows_idx]
    scaled_ratio = scale_factor * weights.astype(jnp.float32) / (samples.astype(jnp.float32)[:, None, None] * row_d[:, :, None] * col_d[:, None, :])
    entries = jnp.log(jnp.maximum(scaled_ratio, 1.0)).astype(jnp.bfloat16).astype(jnp.float32)
    products = jnp.einsum('kij,kjc->kic', entries, picked, precision=lax.Precision.HIGHEST)
    alive_mask = (jnp.arange(capacity, dtype=jnp.int32) < live_count).astype(jnp.float32)
    chooser = (rows_idx[None, :] == jnp.arange(band_blocks, dtype=jnp.int32)[:, None]).astype(jnp.float32) * alive_mask[None, :]
    return running + jnp.einsum('rk,kic->ric', chooser, products, precision=lax.Precision.HIGHEST)

def reference(block_weight, block_row, block_col, block_count, block_samples, row_degree, col_degree, test_matrix):

    def one_band(index):
        r = index // N_BLK
        b = index % N_BLK
        weights = block_weight[r, b]
        running = jnp.zeros((RB_DEV, BLK, SKETCH), jnp.float32)
        for s in range(N_BLK):
            running = tile_update(running, weights[s], block_row[r, b, s], block_col[r, b, s], block_count[r, b, s], block_samples[r, b, s], row_degree[r, b], test_matrix[s], col_degree[s])
        return running
    sketches = lax.map(one_band, jnp.arange(N_ROWS * N_BLK, dtype=jnp.int32))
    flat_rows = sketches.reshape(-1, SKETCH)
    gram_total = jnp.dot(flat_rows.T.astype(jnp.float32), flat_rows.astype(jnp.float32), precision=lax.Precision.HIGHEST, preferred_element_type=jnp.float32)
    lower_factor = jnp.linalg.cholesky(gram_total)
    root = jnp.sqrt(jnp.float32(flat_rows.shape[0]))
    basis_rows = lax.linalg.triangular_solve(lower_factor, flat_rows, left_side=False, lower=True, transpose_a=True) * root
    return (basis_rows.reshape(N_ROWS, N_BLK, BAND, SKETCH), lower_factor.T / root)
```

```python
import functools, jax, jax.numpy as jnp, numpy as np
from jax.sharding import PartitionSpec as P
from jax import lax
from jax.experimental import pallas as pl
from jax.experimental.pallas import tpu as pltpu
F32=jnp.float32; BF16=jnp.bfloat16

def split(x):
    hi = x.astype(BF16)
    return hi, (x - hi.astype(F32)).astype(BF16)

def entries_kernel(row_s, col_s, smp_s, cnt_s, row_v, col_v, cnt_v, w_hbm, rd_ref, cdp_ref, t_ref, s_ref, g_ref, wbuf, ebuf, rinv, cinv, posv, poss, sem, psem):
    copies = [pltpu.make_async_copy(w_hbm.at[pl.ds(i*32,32)], wbuf.at[pl.ds(i*32,32)], sem.at[i]) for i in range(8)]
    for c in copies: c.start()
    kk = lax.broadcasted_iota(jnp.int32, (1,64),1)
    for s in range(4):
        rc = row_v[s:s+1,:]*8 + col_v[s:s+1,:]
        rc = jnp.where(kk < cnt_s[s], rc, -1)
        m = (lax.broadcasted_iota(jnp.int32,(128,64),0) == rc)
        m = jnp.where(m, 1.0, 0.0).astype(BF16)
        kv = jnp.broadcast_to((kk-64), (8,64)).astype(F32).astype(BF16)
        p = lax.dot_general(kv, m, (((1,),(1,)),((),())), preferred_element_type=F32)[0:1]
        p = p.astype(jnp.int32)
        posv[s:s+1,:] = jnp.where(p < 0, p + (64*s+64), 256)
    cp = pltpu.make_async_copy(posv, poss, psem); cp.start()
    r16 = 16.0 / rd_ref[...]
    for q in range(16):
        rinv[q] = jnp.broadcast_to(r16[q:q+1,:], (128,128)).T
    for bc in range(32):
        acc = cdp_ref[bc,0]
        for i in range(1,8): acc = acc + cdp_ref[bc,i]
        cinv[bc] = jnp.broadcast_to(1.0/acc, (8,128))
    ebuf[256] = jnp.zeros((128,128), BF16)
    for s in range(4):
        copies[2*s].wait(); copies[2*s+1].wait()
        def slot(k, _):
            q = row_s[s,k-64*s]; c = col_s[s,k-64*s]
            sm = 1.0 / jnp.full((8,128), smp_s[s,k-64*s], jnp.int32).astype(F32)
            b = cinv[s*8 + c] * sm
            a = rinv[q].reshape(16,8,128)
            w = wbuf[k].astype(F32).reshape(16,8,128)
            e = jnp.log(jnp.maximum(w*a*b[None], 1.0))
            ebuf[k] = e.reshape(128,128).astype(BF16)
            return 0
        lax.fori_loop(64*s, 64*s+64, slot, 0, unroll=2)
    cp.wait()
    def qpair(i, g):
        acc = jnp.zeros((256,128), F32)
        for s in range(4):
            for cp_ in range(4):
                blk=[]
                for dq in range(2):
                    q = 2*i+dq
                    blk.append(jnp.concatenate([ebuf[poss[s, q*8+2*cp_]], ebuf[poss[s, q*8+2*cp_+1]]],axis=1))
                lhs = jnp.concatenate(blk,axis=0)
                acc = acc + jnp.dot(lhs, t_ref[pl.ds((s*4+cp_)*256,256),:], preferred_element_type=F32)
        s_ref[pl.ds(i*256,256),:] = acc
        hi, lo = split(acc)
        return g + lax.dot_general(hi, jnp.concatenate([hi,lo],axis=1), (((0,),(0,)),((),())), preferred_element_type=F32)
    g = lax.fori_loop(0, 8, qpair, jnp.zeros((128,256),F32))
    g_ref[...] = g[:,:128] + g[:,128:] + g[:,128:].T

VM=pl.BlockSpec(memory_space=pltpu.VMEM); SM=pl.BlockSpec(memory_space=pltpu.SMEM); AN=pl.BlockSpec(memory_space=pl.ANY)
def entries(row, col, smp, cnt, w, rd, cdp, t):
    return pl.pallas_call(entries_kernel,
        out_shape=(jax.ShapeDtypeStruct((2048,128),F32), jax.ShapeDtypeStruct((128,128),F32)),
        in_specs=[SM,SM,SM,SM,VM,VM,VM,AN,VM,VM,VM], out_specs=(VM,VM),
        scratch_shapes=[pltpu.VMEM((256,128,128),BF16), pltpu.VMEM((257,128,128),BF16), pltpu.VMEM((16,128,128),F32), pltpu.VMEM((32,8,128),F32),
            pltpu.VMEM((4,128),jnp.int32), pltpu.SMEM((4,128),jnp.int32), pltpu.SemaphoreType.DMA((8,)), pltpu.SemaphoreType.DMA],
        name='entries')(row, col, smp, cnt, row, col, cnt.reshape(1,4), w.reshape(256,128,128), rd.reshape(16,128), cdp, t)

def eliminate(v, n=128):
    sub = lax.broadcasted_iota(jnp.int32,(8,128),0); lane = lax.broadcasted_iota(jnp.int32,(8,128),1)
    for p in range(16):
        P = v[8*p:8*p+8,:]
        for r in range(8):
            j = 8*p+r
            c = jnp.broadcast_to(P[:, j:j+1], (8,128))
            inv = lax.rsqrt(jnp.broadcast_to(c[r:r+1,:],(8,128)))
            row = jnp.where(lane==j, 1.0, jnp.broadcast_to(P[r:r+1,:],(8,128)))*inv
            m = jnp.where(sub>r, c*inv, 0.0)
            P = jnp.where(sub==r, row, jnp.where((lane==j)&(sub>r), 0.0, P) - m*row)
        v[8*p:8*p+8,:] = P
        if p<15:
            lo = 8*p+8
            rhs = jnp.where((lane < lo) & (lane - 8*p > sub), 0.0, P)
            d = lax.dot_general(P, rhs, (((0,),(0,)),((),())), precision=lax.Precision.HIGHEST, preferred_element_type=F32)
            old = v[lo:,:]
            lane2 = lax.broadcasted_iota(jnp.int32, old.shape, 1)
            old = jnp.where((lane2>=8*p)&(lane2<lo), 0.0, old)
            v[lo:,:] = old - d[lo:,:]

def finish_kernel(g_ref, s_ref, b_ref, tri_ref, v):
    v[...] = g_ref[...]
    eliminate(v)
    V = v[...]
    i = lax.broadcasted_iota(jnp.int32,(128,128),0); j = lax.broadcasted_iota(jnp.int32,(128,128),1)
    root = float(np.sqrt(np.float32(524288.0)))
    tri_ref[...] = jnp.where(j>i, V, jnp.where(j==i, 1.0/V, 0.0))*(1.0/root)
    X = jnp.where(j<=i, V, 0.0)*root
    xh, xl = split(X)
    xx = jnp.concatenate([xh,xl],axis=0)
    def step(n,_):
        sh, sl = split(s_ref[pl.ds(n*256,256),:])
        d = lax.dot_general(sh, xx, (((1,),(1,)),((),())), preferred_element_type=F32)
        e = lax.dot_general(sl, xh, (((1,),(1,)),((),())), preferred_element_type=F32)
        b_ref[pl.ds(n*256,256),:] = d[:,:128]+d[:,128:]+e
        return 0
    lax.fori_loop(0,8,step,0)

def finish(g, s):
    return pl.pallas_call(finish_kernel, out_shape=(jax.ShapeDtypeStruct((2048,128),F32), jax.ShapeDtypeStruct((128,128),F32)),
        in_specs=[VM,VM], out_specs=(VM,VM), scratch_shapes=[pltpu.VMEM((128,128),F32)],name='finish')(g,s)
MESH = pl.DeviceIdType.MESH

def place():
    r = lax.axis_index("rows"); b = lax.axis_index("blk")
    return b // 2, lax.rem(b, 2), r // 32, lax.rem(r // 4, 8), lax.rem(r, 4)

def device(y, core, z, x):
    return (lax.rem(y, 2) * 32 + z * 4 + x, (y // 2) * 2 + core)

def greet(peers):
    barrier = pltpu.get_barrier_semaphore()
    for p in peers:
        pl.semaphore_signal(barrier, inc=1, device_id=p, device_id_type=MESH)
    pl.semaphore_wait(barrier, len(peers))

def send(src, dst, ss, rs, dev):
    c = pltpu.make_async_remote_copy(src_ref=src, dst_ref=dst, send_sem=ss, recv_sem=rs, device_id=dev, device_id_type=MESH)
    c.start()
    return c

def axis_peers():
    yh, core, yl, z, x = place()
    y = yh * 2 + yl
    zs = [device(y, core, lax.rem(z + d, 8), x) for d in range(1, 8)]
    ys = [device(lax.rem(y + d, 4), core, z, x) for d in range(1, 4)]
    xs = [device(y, core, z, lax.rem(x + d, 4)) for d in range(1, 4)]
    return zs, ys, xs, device(y, 1 - core, z, x)

def gather_kernel(t_in, cd_in, t_out, cd_out, tb, cb, zs_s, zs_r, b_s, b_r, c_s, c_r, d_s, d_r, l_sem):
    yh, core, yl, z, x = place()
    zp, yp, xp, partner = axis_peers()
    tb[yh, core, yl, z, x] = t_in[...]
    lane = lax.broadcasted_iota(jnp.int32, (1, 128), 1)
    r8 = lax.rem(z, 2) * 4 + x
    cdl = jnp.where(lane // 16 == r8, jnp.concatenate([cd_in[...]] * 8, axis=1), 0.0)
    cb[yh, core, yl, z, x] = cdl
    greet(zp + yp + xp + [partner])
    def both(at, sems_s, sems_r, i, dev):
        return [send(tb.at[at], tb.at[at], sems_s.at[i, 0], sems_r.at[i, 0], dev),
                send(cb.at[at], cb.at[at], sems_s.at[i, 1], sems_r.at[i, 1], dev)]
    A = slice(None)
    cs = []
    for i, p in enumerate(zp):
        cs += both((yh, core, yl, z, x), zs_s, zs_r, i, p)
    for c in cs: c.wait()
    cs = []
    for i in range(3):
        cs += both((yh, core, yl, pl.ds(0, 4), x), b_s, b_r, 2 * i, yp[i])
        cs += both((yh, core, yl, pl.ds(4, 4), A), b_s, b_r, 2 * i + 1, xp[i]) if False else both((yh, core, yl, pl.ds(4, 4), x), b_s, b_r, 2 * i + 1, xp[i])
    for c in cs: c.wait()
    cs = []
    for i in range(3):
        for h in range(2):
            for l in range(2):
                cs += both((h, core, l, pl.ds(0, 4), x), c_s, c_r, 5 * i + 2 * h + l, xp[i])
        cs += both((yh, core, yl, pl.ds(4, 4)), c_s, c_r, 5 * i + 4, yp[i])
    for c in cs: c.wait()
    cs = []
    for h in range(2):
        cs += both((h, core), d_s, d_r, h, partner)
    for c in cs: c.wait()
    o = [pltpu.make_async_copy(tb, t_out, l_sem.at[0]), pltpu.make_async_copy(cb, cd_out, l_sem.at[1])]
    for c in o: c.start()
    for c in o: c.wait()

def gather(t, cd):
    dma = lambda *s: pltpu.SemaphoreType.DMA(s)
    tshape = (2, 2, 2, 8, 4, 16, 128); cshape = (2, 2, 2, 8, 4, 1, 128)
    return pl.pallas_call(gather_kernel, out_shape=(jax.ShapeDtypeStruct(tshape, BF16), jax.ShapeDtypeStruct(cshape, F32)),
        in_specs=[VM, VM], out_specs=(AN, AN),
        scratch_shapes=[pltpu.VMEM(tshape, BF16), pltpu.VMEM(cshape, F32), dma(7,2), dma(7,2), dma(6,2), dma(6,2), dma(15,2), dma(15,2), dma(2,2), dma(2,2), dma(2)],
        compiler_params=pltpu.CompilerParams(collective_id=0, has_side_effects=True), name="gather")(t, cd)

def reduce_phases(g, part, r1, r2, r3, res, s1s, s1r, s2s, s2r, s3s, s3r, s4s, s4r):
    yh, core, yl, z, x = place()
    y = yh * 2 + yl
    own = [x, y]
    def peer(half, d, c):
        return device(y, c, z, lax.rem(x + d, 4)) if half == 0 else device(lax.rem(y + d, 4), c, z, x)
    cs = []
    for half in range(2):
        for d in range(4):
            for dc in range(2):
                if d == 0 and dc == 0: continue
                c2 = lax.rem(core + dc, 2)
                o = lax.rem(own[half] + d, 4)
                cs.append(send(g.at[8 * c2 + 4 * half + o], r1.at[half, 2 * own[half] + core], s1s.at[half, 2 * d + dc], s1r.at[half, 2 * d + dc], peer(half, d, c2)))
        r1[half, 2 * own[half] + core] = g[8 * core + 4 * half + own[half]]
    for c in cs: c.wait()
    cs = []
    for half in range(2):
        a = r1[half, 0]
        for i in range(1, 8): a = a + r1[half, i]
        other = own[1 - half]
        r2[half, other] = a
        for d in range(1, 4):
            cs.append(send(r2.at[half, other], r2.at[half, other], s2s.at[half, d - 1], s2r.at[half, d - 1], peer(1 - half, d, core)))
    for c in cs: c.wait()
    for half in range(2):
        r3[z, half] = (r2[half, 0] + r2[half, 1]) + (r2[half, 2] + r2[half, 3])
    cs = []
    for d in range(1, 8):
        cs.append(send(r3.at[z], r3.at[z], s3s.at[d - 1], s3r.at[d - 1], device(y, core, lax.rem(z + d, 8), x)))
    for c in cs: c.wait()
    cs = []
    for half in range(2):
        a = ((r3[0, half] + r3[1, half]) + (r3[2, half] + r3[3, half])) + ((r3[4, half] + r3[5, half]) + (r3[6, half] + r3[7, half]))
        at = 8 * core + 4 * half + own[half]
        res[at] = a
        for d in range(4):
            for dc in range(2):
                if d == 0 and dc == 0: continue
                cs.append(send(res.at[at], res.at[at], s4s.at[half, 2 * d + dc], s4r.at[half, 2 * d + dc], peer(half, d, lax.rem(core + dc, 2))))
    for c in cs: c.wait()

def reduce_kernel(g, out, part, r1, r2, r3, res, *sems):
    yh, core, yl, z, x = place()
    y = yh * 2 + yl
    zp, yp, xp, partner = axis_peers()
    other = [device(lax.rem(y + d, 4), 1 - core, z, x) for d in range(1, 4)] + [device(y, 1 - core, z, lax.rem(x + d, 4)) for d in range(1, 4)]
    greet(zp + yp + xp + [partner] + other)
    reduce_phases(g, part, r1, r2, r3, res, *sems)
    out[...] = res[...]

def reduce_scratch():
    dma = lambda *s: pltpu.SemaphoreType.DMA(s)
    return [pltpu.VMEM((2,8,128),F32), pltpu.VMEM((2,8,8,128),F32), pltpu.VMEM((2,4,8,128),F32), pltpu.VMEM((8,2,8,128),F32), pltpu.VMEM((16,8,128),F32),
            dma(2,8),dma(2,8),dma(2,3),dma(2,3),dma(7),dma(7),dma(2,8),dma(2,8)]

def reduce_gram(g):
    return pl.pallas_call(reduce_kernel, out_shape=jax.ShapeDtypeStruct((16,8,128),F32), in_specs=[VM], out_specs=VM,
        scratch_shapes=reduce_scratch(), compiler_params=pltpu.CompilerParams(collective_id=1, has_side_effects=True), name="reduce")(g.reshape(16,8,128)).reshape(128,128)

def body(w, row, col, cnt, smp, rd, cd, t):
    tt, cc = gather(t[0], cd)
    s, g = entries(row[0,0], col[0,0], smp[0,0], cnt[0,0], w[0,0], rd[0,0], cc.reshape(32,8,1,128), tt.reshape(4096,128))
    g = reduce_gram(g)
    b, tri = finish(g, s)
    return b.reshape(1,1,2048,128), tri

def solution(mesh):
    placed = (P("rows","blk",None,None,None,None), P("rows","blk",None,None), P("rows","blk",None,None), P("rows","blk",None), P("rows","blk",None,None), P("rows","blk",None), P("blk","rows"), P("blk","rows",None))
    return jax.shard_map(body, mesh=mesh, in_specs=placed, out_specs=(P("rows","blk",None,None), P()), check_vma=False)
```

```python
import numpy as np
import jax
import jax.numpy as jnp
from jax import lax
from jax.experimental import pallas as pl
from jax.experimental.pallas import tpu as pltpu
from jax.sharding import PartitionSpec as P

F32 = jnp.float32
BF16 = jnp.bfloat16
MESH = pl.DeviceIdType.MESH
VM = pl.BlockSpec(memory_space=pltpu.VMEM)
SM = pl.BlockSpec(memory_space=pltpu.SMEM)
AN = pl.BlockSpec(memory_space=pl.ANY)
A = slice(None)


def dma(*shape):
    return pltpu.SemaphoreType.DMA(shape)


def split2(x):
    hi = x.astype(BF16)
    return hi, (x - hi.astype(F32)).astype(BF16)


def split3(x):
    h = x.astype(BF16)
    r = x - h.astype(F32)
    m = r.astype(BF16)
    return h, m, (r - m.astype(F32)).astype(BF16)


def place():
    r = lax.axis_index("rows")
    b = lax.axis_index("blk")
    return b // 2, lax.rem(b, 2), r // 32, lax.rem(r // 4, 8), lax.rem(r, 4)


def device(y, core, z, x):
    return (lax.rem(y, 2) * 32 + z * 4 + x, (y // 2) * 2 + core)


def send(src, dst, ss, rs, dev):
    c = pltpu.make_async_remote_copy(
        src_ref=src, dst_ref=dst, send_sem=ss, recv_sem=rs, device_id=dev, device_id_type=MESH
    )
    c.start()
    return c


def wait_all(copies):
    for c in copies:
        c.wait()


def slot_table(row_v, col_v, cnt_s, posv):
    kk = lax.broadcasted_iota(jnp.int32, (1, 64), 1)
    lane = lax.broadcasted_iota(jnp.int32, (64, 128), 1)
    slot = lax.broadcasted_iota(jnp.int32, (64, 128), 0) + 1
    for s in range(4):
        rc = jnp.where(kk < cnt_s[s], row_v[s : s + 1, :] * 8 + col_v[s : s + 1, :], -1)
        rc = jnp.broadcast_to(jnp.concatenate([rc, rc], axis=1), (128, 128)).T[0:64]
        p = jnp.sum(jnp.where(rc == lane, slot, 0), axis=0, keepdims=True)
        posv[s : s + 1, :] = jnp.clip(jnp.where(p > 0, p + (64 * s - 1), 256), 0, 256)


def row_logs(rd_ref, rlog):
    r16 = jnp.log(16.0 / rd_ref[...])
    for q in range(16):
        rlog[q] = jnp.broadcast_to(r16[q : q + 1, :], (128, 128)).T


def weight_logs(s, wbuf, row_s, smp_s, rlog, ubuf):
    def slot(k, carry):
        n = jnp.log(jnp.full((8, 128), smp_s[s, k - 64 * s], jnp.int32).astype(F32))
        a = rlog[row_s[s, k - 64 * s]].reshape(16, 8, 128)
        w = wbuf[k].astype(F32).reshape(16, 8, 128)
        ubuf[k] = (jnp.log(w) + (a - n[None])).reshape(128, 128)
        return carry

    lax.fori_loop(64 * s, 64 * s + 64, slot, 0, unroll=2)


def group_products(first, yh, core, yl, ubuf, poss, tb, cb, sk):
    s = 2 * yh + core
    clog = []
    for c in range(4):
        acc = None
        for i in range(8):
            v = cb[yh, core, yl, 2 * c + i // 4, i % 4]
            acc = v if acc is None else acc + v
        clog.append(jnp.broadcast_to(jnp.log(acc), (8, 128)))

    def block(q, c):
        u = ubuf[poss[s, q * 8 + yl * 4 + c]].reshape(16, 8, 128)
        return jnp.maximum(u - clog[c][None], 0.0).reshape(128, 128).astype(BF16)

    def rows(i, carry):
        acc = None
        for c in range(2):
            e = [jnp.concatenate([block(2 * i + dq, 2 * c), block(2 * i + dq, 2 * c + 1)], axis=1) for dq in range(2)]
            t = tb[yh, core, yl, pl.ds(4 * c, 4)].reshape(256, 128)
            d = jnp.dot(jnp.concatenate(e, axis=0), t, preferred_element_type=F32)
            acc = d if acc is None else acc + d
        at = pl.ds(i * 256, 256)
        sk[at, :] = acc if first else sk[at, :] + acc
        return carry

    lax.fori_loop(0, 8, rows, 0, unroll=2)


def gram_sum(g, r1, r2, r3, res, s1s, s1r, s2s, s2r, s3s, s3r, s4s, s4r):
    yh, core, yl, z, x = place()
    y = yh * 2 + yl
    own = [x, y]

    def peer(half, d, c):
        if half == 0:
            return device(y, c, z, lax.rem(x + d, 4))
        return device(lax.rem(y + d, 4), c, z, x)

    cs = []
    for d, dc in [(d, dc) for d in (2, 1, 3, 0) for dc in range(2) if d + dc]:
        for half in range(2):
            c2 = lax.rem(core + dc, 2)
            o = lax.rem(own[half] + d, 4)
            i = 2 * d + dc
            cs.append(
                send(
                    g.at[8 * c2 + 4 * half + o],
                    r1.at[half, 2 * own[half] + core],
                    s1s.at[half, i],
                    s1r.at[half, i],
                    peer(half, d, c2),
                )
            )
    for half in range(2):
        r1[half, 2 * own[half] + core] = g[8 * core + 4 * half + own[half]]
    wait_all(cs)
    cs = []
    for half in range(2):
        a = [r1[half, i] for i in range(8)]
        other = own[1 - half]
        r2[half, other] = ((a[0] + a[1]) + (a[2] + a[3])) + ((a[4] + a[5]) + (a[6] + a[7]))
    for d in (2, 1, 3):
        for half in range(2):
            other = own[1 - half]
            at = r2.at[half, other]
            cs.append(send(at, at, s2s.at[half, d - 1], s2r.at[half, d - 1], peer(1 - half, d, core)))
    wait_all(cs)
    for half in range(2):
        r3[z, half] = (r2[half, 0] + r2[half, 1]) + (r2[half, 2] + r2[half, 3])
    cs = []
    for d in (4, 3, 5, 2, 6, 1, 7):
        cs.append(send(r3.at[z], r3.at[z], s3s.at[d - 1], s3r.at[d - 1], device(y, core, lax.rem(z + d, 8), x)))
    wait_all(cs)
    cs = []
    for half in range(2):
        a = [r3[i, half] for i in range(8)]
        res[8 * core + 4 * half + own[half]] = ((a[0] + a[1]) + (a[2] + a[3])) + ((a[4] + a[5]) + (a[6] + a[7]))
    for d, dc in [(d, dc) for d in (2, 1, 3, 0) for dc in range(2) if d + dc]:
        for half in range(2):
            at = res.at[8 * core + 4 * half + own[half]]
            i = 2 * d + dc
            cs.append(send(at, at, s4s.at[half, i], s4r.at[half, i], peer(half, d, lax.rem(core + dc, 2))))
    wait_all(cs)


def sketch_kernel(
    row_s, col_s, smp_s, cnt_s, row_v, col_v, rd_ref, cd_ref, t_ref, w_hbm,
    s_out, g_out,
    wbuf, ubuf, rlog, posv, poss, tb, cb, sk, g, r1, r2, r3, res,
    w_sem, p_sem, o_sem, z_s, z_r, a_s, a_r, d_s, d_r, *red_sems,
):
    yh, core, yl, z, x = place()
    y = yh * 2 + yl
    partner = device(y, 1 - core, z, x)
    zp = {d: device(y, core, lax.rem(z + d, 8), x) for d in range(1, 8)}
    plane = {
        (dy, dx): device(lax.rem(y + dy, 4), core, z, lax.rem(x + dx, 4))
        for dy in range(4) for dx in range(4) if dy + dx
    }
    across = [device(lax.rem(y + d, 4), 1 - core, z, x) for d in range(1, 4)]
    across += [device(y, 1 - core, z, lax.rem(x + d, 4)) for d in range(1, 4)]
    barrier = pltpu.get_barrier_semaphore()
    greeted = list(zp.values()) + list(plane.values()) + across + [partner]
    for p in greeted:
        pl.semaphore_signal(barrier, inc=1, device_id=p, device_id_type=MESH)
    loads = [pltpu.make_async_copy(w_hbm.at[pl.ds(i * 32, 32)], wbuf.at[pl.ds(i * 32, 32)], w_sem.at[i]) for i in range(8)]
    for c in loads:
        c.start()
    tb[yh, core, yl, z, x] = t_ref[0]
    lane = lax.broadcasted_iota(jnp.int32, (1, 128), 1)
    cb[yh, core, yl, z, x] = jnp.where(
        lane // 16 == lax.rem(z, 2) * 4 + x, jnp.concatenate([cd_ref[...]] * 8, axis=1), 0.0
    )
    slot_table(row_v, col_v, cnt_s, posv)
    to_scalars = pltpu.make_async_copy(posv, poss, p_sem)
    to_scalars.start()
    row_logs(rd_ref, rlog)
    ubuf[256] = jnp.full((128, 128), -1e30, F32)
    pl.semaphore_wait(barrier, len(greeted))

    def move(buf, n, ss, rs, i, at, dev):
        return send(buf.at[at], buf.at[at], ss.at[n, i], rs.at[n, i], dev)

    both = ((cb, 0), (tb, 1))
    own = (yh, core, yl, z, x)
    c1 = [move(buf, n, z_s, z_r, d - 1, own, zp[d]) for buf, n in both for d in (4, 3, 5, 2, 6, 1, 7)]
    for c in loads[0:4]:
        c.wait()
    weight_logs(0, wbuf, row_s, smp_s, rlog, ubuf)
    weight_logs(1, wbuf, row_s, smp_s, rlog, ubuf)
    wait_all(c1)
    column = (yh, core, yl, A, x)
    order = (0, 1, 3, 2)
    c2 = {
        dy: [
            move(buf, n, a_s, a_r, 4 * dy + dx, column, plane[dy, dx])
            for buf, n in both for dx in (2, 1, 3, 0) if dy + dx
        ]
        for dy in order
    }
    for c in loads[4:8]:
        c.wait()
    weight_logs(2, wbuf, row_s, smp_s, rlog, ubuf)
    weight_logs(3, wbuf, row_s, smp_s, rlog, ubuf)
    to_scalars.wait()
    c3 = {}
    first = True
    for dy in order:
        yg = lax.rem(y + 4 - dy, 4)
        for c in c2[dy]:
            c.wait_recv()
        at = (yg // 2, core, lax.rem(yg, 2))
        c3[dy] = [move(buf, n, d_s, d_r, dy, at, partner) for buf, n in both]
        group_products(first, at[0], core, at[2], ubuf, poss, tb, cb, sk)
        first = False
    for dy in order:
        yg = lax.rem(y + 4 - dy, 4)
        for c in c3[dy]:
            c.wait_recv()
        group_products(False, yg // 2, 1 - core, lax.rem(yg, 2), ubuf, poss, tb, cb, sk)
    out = pltpu.make_async_copy(sk, s_out, o_sem)
    out.start()
    gacc = None
    for i in range(2):
        hi, lo = split2(sk[pl.ds(i * 1024, 1024), :])
        d = lax.dot_general(
            hi, jnp.concatenate([hi, lo], axis=1), (((0,), (0,)), ((), ())), preferred_element_type=F32
        )
        gacc = d if gacc is None else gacc + d
    g[...] = (gacc[:, :128] + gacc[:, 128:] + gacc[:, 128:].T).reshape(16, 8, 128)
    gram_sum(g, r1, r2, r3, res, *red_sems)
    g_out[...] = res[...].reshape(128, 128)
    out.wait()
    for dy in order:
        for c in c2[dy] + c3[dy]:
            c.wait_send()


def sketch(w, row, col, cnt, smp, rd, cd, t):
    tshape = (2, 2, 2, 8, 4, 16, 128)
    cshape = (2, 2, 2, 8, 4, 1, 128)
    vm = pltpu.VMEM
    return pl.pallas_call(
        sketch_kernel,
        out_shape=(jax.ShapeDtypeStruct((2048, 128), F32), jax.ShapeDtypeStruct((128, 128), F32)),
        in_specs=[SM] * 4 + [VM] * 5 + [AN],
        out_specs=(AN, VM),
        scratch_shapes=[
            vm((256, 128, 128), BF16), vm((257, 128, 128), F32), vm((16, 128, 128), F32),
            vm((4, 128), jnp.int32), pltpu.SMEM((4, 128), jnp.int32),
            vm(tshape, BF16), vm(cshape, F32), vm((2048, 128), F32), vm((16, 8, 128), F32),
            vm((2, 8, 8, 128), F32), vm((2, 4, 8, 128), F32), vm((8, 2, 8, 128), F32), vm((16, 8, 128), F32),
            dma(8), dma(), dma(),
            dma(2, 7), dma(2, 7), dma(2, 16), dma(2, 16), dma(2, 4), dma(2, 4),
            dma(2, 8), dma(2, 8), dma(2, 3), dma(2, 3), dma(7), dma(7), dma(2, 8), dma(2, 8),
        ],
        compiler_params=pltpu.CompilerParams(collective_id=0, has_side_effects=True),
        name="sketch",
    )(row, col, smp, cnt, row, col, rd.reshape(16, 128), cd, t, w.reshape(256, 128, 128))


def bl(v, j):
    return jnp.broadcast_to(v[:, j : j + 1], v.shape)


def bs(v, r):
    return jnp.broadcast_to(v[r : r + 1, :], v.shape)


def pick(rows, sub):
    out = rows[7]
    for r in range(6, -1, -1):
        out = jnp.where(sub == r, rows[r], out)
    return out


def factor_panel(panel, p, sub, lane):
    lo = 8 * p
    cols = [bl(panel, lo + k) for k in range(8)]
    a = {(i, k): bs(cols[k], i) for k in range(8) for i in range(k, 8)}
    inside = (lane >= lo) & (lane < lo + 8)
    z = [bs(panel, r) for r in range(8)]
    y = [jnp.where(inside, jnp.where(lane == lo + r, 1.0, 0.0), z[r]) for r in range(8)]
    for k in range(8):
        inv = lax.rsqrt(a[k, k])
        y[k] = y[k] * inv
        z[k] = z[k] * inv
        f = {i: a[i, k] * inv for i in range(k + 1, 8)}
        for i in range(k + 1, 8):
            for j in range(k + 1, i + 1):
                a[i, j] = a[i, j] - f[i] * f[j]
            y[i] = y[i] - f[i] * y[k]
            z[i] = z[i] - f[i] * z[k]
    return pick(y, sub), pick(z, sub)


def factor(g, v, u):
    sub = lax.broadcasted_iota(jnp.int32, (8, 128), 0)
    lane = lax.broadcasted_iota(jnp.int32, (8, 128), 1)
    rows = [g[8 * t : 8 * t + 8, :] for t in range(16)]
    for p in range(16):
        yv, zv = factor_panel(rows[p], p, sub, lane)
        v[8 * p : 8 * p + 8, :] = yv
        u[8 * p : 8 * p + 8, :] = zv
        if p == 15:
            break
        keep = (lane >= 8 * p) & (lane < 8 * p + 8)
        new = []
        for i in range(8):
            e = bl(yv, 8 * p + 8 + i) * yv
            e = e + pltpu.roll(e, 4, 0)
            e = e + pltpu.roll(e, 2, 0)
            new.append(e + pltpu.roll(e, 1, 0))
        rows[p + 1] = jnp.where(keep, 0.0, rows[p + 1]) - pick(new, sub)
        if p < 14:
            h, m, l = split3(yv)
            d = lax.dot_general(
                jnp.concatenate([h, h, m, m, h, l], axis=0),
                jnp.concatenate([h, m, h, m, l, h], axis=0),
                (((0,), (0,)), ((), ())),
                preferred_element_type=F32,
            )
            for t in range(p + 2, 16):
                rows[t] = jnp.where(keep, 0.0, rows[t]) - d[8 * t : 8 * t + 8, :]


def basis_kernel(g_ref, s_hbm, b_hbm, tri_ref, v, u, sk, bs_, i_sem, o_sem):
    load = pltpu.make_async_copy(s_hbm, sk, i_sem)
    load.start()
    factor(g_ref, v, u)
    i = lax.broadcasted_iota(jnp.int32, (128, 128), 0)
    j = lax.broadcasted_iota(jnp.int32, (128, 128), 1)
    root = float(np.sqrt(np.float32(524288.0)))
    tri_ref[...] = jnp.where(j >= i, u[...], 0.0) * (1.0 / root)
    xh, xl = split2(jnp.where(j <= i, v[...], 0.0) * root)
    xx = jnp.concatenate(
        [jnp.concatenate([xh, xh], axis=1), jnp.concatenate([xl, jnp.zeros_like(xl)], axis=1)], axis=0
    )
    load.wait()
    outs = []
    for n in range(8):
        at = pl.ds(n * 256, 256)
        sh, sl = split2(sk[n * 256 : n * 256 + 256, :])
        d = lax.dot_general(
            jnp.concatenate([sh, sl], axis=1), xx, (((1,), (1,)), ((), ())), preferred_element_type=F32
        )
        bs_[n * 256 : n * 256 + 256, :] = d[:, :128] + d[:, 128:]
        c = pltpu.make_async_copy(bs_.at[at], b_hbm.at[at], o_sem.at[n])
        c.start()
        outs.append(c)
    wait_all(outs)


def basis(g, s):
    return pl.pallas_call(
        basis_kernel,
        out_shape=(jax.ShapeDtypeStruct((2048, 128), F32), jax.ShapeDtypeStruct((128, 128), F32)),
        in_specs=[VM, AN],
        out_specs=(AN, VM),
        scratch_shapes=[pltpu.VMEM((128, 128), F32)] * 2 + [pltpu.VMEM((2048, 128), F32)] * 2 + [dma(), dma(8)],
        name="basis",
    )(g, s)


def body(w, row, col, cnt, smp, rd, cd, t):
    s, g = sketch(w[0, 0], row[0, 0], col[0, 0], cnt[0, 0], smp[0, 0], rd[0, 0], cd, t)
    b, tri = basis(g, s)
    return b.reshape(1, 1, 2048, 128), tri


def solution(mesh):
    placed = (
        P("rows", "blk", None, None, None, None),
        P("rows", "blk", None, None),
        P("rows", "blk", None, None),
        P("rows", "blk", None),
        P("rows", "blk", None, None),
        P("rows", "blk", None),
        P("blk", "rows"),
        P("blk", "rows", None),
    )
    return jax.shard_map(
        body, mesh=mesh, in_specs=placed, out_specs=(P("rows", "blk", None, None), P()), check_vma=False
    )
```
